256 devices in a mesh: epoch: 16 (over x, y), row: 16 (over z, core).
Axes of the slice: x: 4, y: 4, z: 8, core: 2. Of those that a mesh axis runs over, the one named last changes fastest.
Arguments:
- forcing: float32 [16, 2, 128, 6144], P('epoch', None, 'row'), may hold values from -2400 to 2400
- observed: float32 [16, 2, 128, 6144], P('epoch', None, 'row'), may hold values from -6 to 6
- log_friction: float32 [128, 6144], P('row'), may hold values from -1.5 to 1.5
- log_rheology: float32 [128, 6144], P('row'), may hold values from -0.7 to 0.7
- grounded: int32 [128, 6144], P('row'), may hold values 0 or 1
Outputs:
- new_friction: float32 [128, 6144], P('row')
- new_rheology: float32 [128, 6144], P('row')
The draws below stay inside these ranges and needn't reach their ends.
All inputs are finite; a program needn't handle non-finite values. No bound on the sum of `grounded` on one device may be relied on, other than what follows from the above.
Results may differ from the reference program's by a relative error of at most 0.00011.
Values sent between devices are 32-bit elements; how exact they have to be, the bound alone decides.
A program may use at most 64 MiB of HBM per device.

```python
import math
import jax
import jax.numpy as jnp
from jax import lax

COLS = 6144
SWEEPS = 4
EPOCHS = 16
NROWS = 128


def draw_forcing(key, part):
    key_base, key_rows, key_cols = jax.random.split(key, 3)
    shape = (EPOCHS, 2, NROWS, COLS)
    base = jax.random.truncated_normal(key_base, -4.0, 4.0, shape, jnp.float32)
    rising = 2.0
    row_place = jnp.arange(NROWS, dtype=jnp.float32) / max(NROWS - 1, 1)
    row_factor = jnp.exp(jax.random.uniform(key_rows, (NROWS,), jnp.float32, 0.0, math.log(10.0))) * (1.0 + rising * row_place)
    col_factor = jnp.exp(jax.random.uniform(key_cols, (COLS,), jnp.float32, 0.0, math.log(10.0)))
    epoch_factor = 1.0 + jnp.arange(EPOCHS, dtype=jnp.float32) / max(EPOCHS - 1, 1)
    return 0.5 * base * epoch_factor[:, None, None, None] * row_factor[:, None] * col_factor[None, :]


def place_ends(result, key, smallest, top_value):
    spot = [jax.random.randint(jax.random.fold_in(key, axis), (), 0, length) for axis, length in enumerate(result.shape)]
    main_axis = result.shape.index(max(result.shape))
    beside = spot[:main_axis] + [(spot[main_axis] + 1) % result.shape[main_axis]] + spot[main_axis + 1:]
    return result.at[tuple(spot)].set(smallest).at[tuple(beside)].set(top_value)


def block_levels(key, dims, cuts, least, largest):
    def one(axis_at, blocks):
        heights = jax.random.uniform(jax.random.fold_in(jax.random.fold_in(key, 6), axis_at), (blocks,), jnp.float32, least / len(cuts), largest / len(cuts))
        return jnp.repeat(jnp.exp(heights), dims[axis_at] // blocks).reshape((-1,) + (1,) * (len(dims) - axis_at - 1))

    factor_of = one(*cuts[0])
    for cut in cuts[1:]:
        factor_of = factor_of * one(*cut)
    return factor_of


def bell_draw(rng, extent, spread, most, cuts=(), kind=jnp.bfloat16):
    values = jax.random.normal(rng, extent, jnp.float32) * spread
    if len(cuts) > 0:
        values = block_levels(rng, extent, cuts, -0.22, 0.18) * values
    return jnp.clip(values, min=-most, max=most).astype(kind)


def setup_inputs(seed: int = 0) -> dict:
    streams_of = jax.random.split(jax.random.key(seed), 6)
    return {
        "forcing": draw_forcing(jax.random.fold_in(streams_of[5], 71), 0),
        "observed": bell_draw(streams_of[1], (EPOCHS, 2, NROWS, COLS), 1.0, 6.0, ((0, 16), (2, 16)), jnp.float32),
        "log_friction": jnp.clip(jax.random.uniform(streams_of[2], (NROWS, COLS), jnp.float32, -1.5, 1.5) * block_levels(streams_of[2], (NROWS, COLS), ((0, 16),), -0.4, 0.0), -1.5, 1.5),
        "log_rheology": jnp.clip(jax.random.uniform(streams_of[3], (NROWS, COLS), jnp.float32, -0.7, 0.7) * block_levels(streams_of[3], (NROWS, COLS), ((0, 16),), -0.4, 0.0), -0.7, 0.7),
        "grounded": place_ends((jax.random.randint(streams_of[4], (NROWS, COLS), 0, 4) < 3).astype(jnp.int32), jax.random.fold_in(streams_of[4], 1), 0, 1),
    }


relax = 0.9
coupling = 0.1
step_size = 0.5

def shift_east(field):
    widths = [(0, 0)] * (field.ndim - 1) + [(0, 1)]
    return jnp.pad(field[..., 1:], widths)

def shift_west(field):
    widths = [(0, 0)] * (field.ndim - 1) + [(1, 0)]
    return jnp.pad(field[..., :-1], widths)

def cross_term(padded_comp):
    return shift_east(padded_comp[2:]) - shift_west(padded_comp[2:]) - shift_east(padded_comp[:-2]) + shift_west(padded_comp[:-2])

def pad_rows(field):
    widths = [(0, 0)] * (field.ndim - 2) + [(1, 1), (0, 0)]
    return jnp.pad(field, widths)

def jacobi_sweep(padded_velocity, padded_stiffness, friction_coef, forcing_now):
    centre = padded_stiffness[1:-1]
    face_east = 0.5 * (centre + shift_east(centre))
    face_west = 0.5 * (centre + shift_west(centre))
    face_north = 0.5 * (centre + padded_stiffness[:-2])
    face_south = 0.5 * (centre + padded_stiffness[2:])
    along_sum = face_east + face_west
    across = face_north + face_south
    diag_u = 4.0 * along_sum + across + friction_coef + 0.5
    diag_v = along_sum + 4.0 * across + friction_coef + 0.5
    padded_u = padded_velocity[0]
    padded_v = padded_velocity[1]
    inner_u = padded_u[1:-1]
    inner_v = padded_v[1:-1]
    lateral_u = face_east * shift_east(inner_u) + face_west * shift_west(inner_u)
    vertical_u = face_north * padded_u[:-2] + face_south * padded_u[2:]
    lateral_v = face_east * shift_east(inner_v) + face_west * shift_west(inner_v)
    vertical_v = face_north * padded_v[:-2] + face_south * padded_v[2:]
    image_u = diag_u * inner_u - 4.0 * lateral_u - vertical_u - coupling * centre * cross_term(padded_v)
    image_v = diag_v * inner_v - lateral_v - 4.0 * vertical_v - coupling * centre * cross_term(padded_u)
    new_u = inner_u + relax * (forcing_now[0] - image_u) / diag_u
    new_v = inner_v + relax * (forcing_now[1] - image_v) / diag_v
    return jnp.stack([new_u, new_v])

def reference(forcing, observed, log_friction, log_rheology, grounded):
    stiffness = jnp.exp(log_rheology)
    friction_coef = grounded.astype(jnp.float32) * jnp.exp(log_friction)

    def one_epoch(running, epoch_data):
        forcing_now, target = epoch_data

        def forward(stiff_field, friction_field):
            velocity = jnp.zeros(forcing_now.shape, jnp.float32)
            padded_stiffness = pad_rows(stiff_field)
            for sweep_index in range(SWEEPS):
                velocity = jacobi_sweep(pad_rows(velocity), padded_stiffness, friction_field, forcing_now)
            return velocity
        velocity, pullback = jax.vjp(forward, stiffness, friction_coef)
        grad_stiff, grad_friction = pullback(velocity - target)
        return ((running[0] + grad_stiff, running[1] + grad_friction), None)
    zeros_field = jnp.zeros(stiffness.shape, jnp.float32)
    (grad_stiff, grad_friction), unused = lax.scan(one_epoch, (zeros_field, zeros_field), (forcing, observed))
    gradient = jnp.stack([grad_friction * friction_coef, grad_stiff * stiffness])
    parameters = jnp.stack([log_friction, log_rheology])
    grad_scale = jnp.sqrt(lax.optimization_barrier(jnp.mean(gradient * gradient, axis=(1, 2))) + 1e-06)
    updated = parameters - step_size * gradient / grad_scale[:, None, None]
    return (updated[0], updated[1])
```

```python
import math

import jax
import jax.numpy as jnp
from jax import lax
from jax.experimental import pallas as pl
from jax.experimental.pallas import tpu as pltpu
from jax.sharding import PartitionSpec as P

relax = 0.9
coupling = 0.1
step_size = 0.5
keep = 1.0 - relax

MESH = pl.DeviceIdType.MESH
ROWS = 8
OFF = 4
HELD = ROWS + 2 * OFF
SUB, LANE = 8, 128


def make_kernel(n_epoch, n_row, cols):
    pieces = cols // (SUB * LANE)
    span = pieces * SUB
    side = math.isqrt(n_epoch)
    cells = n_row * ROWS * cols

    def kernel(
        f_in, o_in, lf_in, lr_in, gr_in, outq, outr,
        fraw, oraw, lfraw, lrraw, grraw,
        stiff, fric, force, fe, fw, fn, fs, m01, rdu, rdv,
        v1, v2, v3, v4,
        l4, p4, q4, l3, p3, q3, l2, p2, q2,
        accn, accs, acce, accw, accc, accu, accv,
        facen, faces, own, grad, g4out, g4in,
        rsbuf, summed, total, sqout, sqin, rowout, rowin,
        load_sem, hsend, hrecv, asend, arecv, rsend, rrecv, gsend, grecv, ssend, srecv, tsend, trecv,
    ):
        me = lax.axis_index("row")
        ep = lax.axis_index("epoch")
        up = lax.rem(me + n_row - 1, n_row)
        down = lax.rem(me + 1, n_row)
        has_up = (me > 0).astype(jnp.float32)
        has_down = (me < n_row - 1).astype(jnp.float32)

        loads = [
            pltpu.make_async_copy(src, dst, load_sem.at[k])
            for k, (src, dst) in enumerate(
                ((lr_in, lrraw), (lf_in, lfraw), (gr_in, grraw), (f_in, fraw), (o_in, oraw))
            )
        ]
        for load in loads:
            load.start()

        ex, ey = ep // side, lax.rem(ep, side)
        peers = []
        for dx in range(side):
            for dy in range(side):
                if dx or dy:
                    peers.append(lax.rem(ex + dx, side) * side + lax.rem(ey + dy, side))

        barrier = pltpu.get_barrier_semaphore()
        for k in range(1, n_row):
            pl.semaphore_signal(
                barrier, inc=1, device_id={"row": lax.rem(me + k, n_row)}, device_id_type=MESH
            )
        for peer in peers:
            pl.semaphore_signal(barrier, inc=1, device_id={"epoch": peer}, device_id_type=MESH)

        lane = lax.broadcasted_iota(jnp.int32, (SUB, LANE), 1)
        sub = lax.broadcasted_iota(jnp.int32, (SUB, LANE), 0)
        last_lane, first_lane = lane == LANE - 1, lane == 0
        last_sub, first_sub = sub == SUB - 1, sub == 0
        zero = jnp.zeros((SUB, LANE), jnp.float32)
        every = range(pieces)

        def east(x):
            r = [pltpu.roll(p, LANE - 1, 1) for p in x]
            end = jnp.where(last_sub, zero, pltpu.roll(r[0], SUB - 1, 0))
            return [jnp.where(last_lane, r[k + 1] if k + 1 < pieces else end, r[k]) for k in every]

        def west(x):
            r = [pltpu.roll(p, 1, 1) for p in x]
            end = jnp.where(first_sub, zero, pltpu.roll(r[-1], 1, 0))
            return [jnp.where(first_lane, r[k - 1] if k else end, r[k]) for k in every]

        def lanes(k):
            return slice(k * LANE, (k + 1) * LANE)

        def get(ref, *at):
            return [ref[(*at, slice(None), lanes(k))] for k in every]

        def put(ref, x, *at):
            for k in every:
                ref[(*at, slice(None), lanes(k))] = x[k]

        def raw(ref, i, part=0):
            return [ref[pl.ds(part * span * SUB + k * SUB + i, SUB, stride=span), :] for k in every]

        def cross(north, south):
            d = [s - n for s, n in zip(south, north)]
            return [a - b for a, b in zip(east(d), west(d))]

        def rows(lo, hi, body):
            def step(a, carry):
                body(a)
                return carry

            lax.fori_loop(lo + OFF, hi + OFF, step, 0)

        loads[0].wait()

        def own_stiff(a):
            put(stiff, [jnp.exp(x) for x in raw(lrraw, a - OFF)], a)

        rows(0, ROWS, own_stiff)
        loads[1].wait()
        loads[2].wait()

        def own_fric(a):
            held_up = zip(raw(grraw, a - OFF), raw(lfraw, a - OFF))
            put(fric, [g.astype(jnp.float32) * jnp.exp(x) for g, x in held_up], a)

        rows(0, ROWS, own_fric)
        loads[3].wait()

        def own_force(a):
            put(force, raw(fraw, a - OFF, 0), a, 0)
            put(force, raw(fraw, a - OFF, 1), a, 1)

        rows(0, ROWS, own_force)

        pl.semaphore_wait(barrier, n_row - 1 + len(peers))

        def send(src, dst, ssem, rsem, where):
            copy = pltpu.make_async_remote_copy(
                src_ref=src, dst_ref=dst, send_sem=ssem, recv_sem=rsem,
                device_id=where, device_id_type=MESH,
            )
            copy.start()
            return copy

        halo = []
        for k, (ref, depth) in enumerate(((stiff, 4), (fric, 3), (force, 3))):
            halo.append(send(
                ref.at[pl.ds(OFF, depth)], ref.at[pl.ds(OFF + ROWS, depth)],
                hsend.at[2 * k], hrecv.at[2 * k], {"row": up},
            ))
            halo.append(send(
                ref.at[pl.ds(OFF + ROWS - depth, depth)], ref.at[pl.ds(OFF - depth, depth)],
                hsend.at[2 * k + 1], hrecv.at[2 * k + 1], {"row": down},
            ))

        def coefficients(a):
            c, n, s = get(stiff, a), get(stiff, a - 1), get(stiff, a + 1)
            he = [0.5 * (x + y) for x, y in zip(c, east(c))]
            hw = [0.5 * (x + y) for x, y in zip(c, west(c))]
            hn = [0.5 * (x + y) for x, y in zip(c, n)]
            hs = [0.5 * (x + y) for x, y in zip(c, s)]
            fr = get(fric, a)
            inside = relax * jnp.where(a < OFF, has_up, jnp.where(a >= OFF + ROWS, has_down, 1.0))
            put(fe, he, a)
            put(fw, hw, a)
            put(fn, hn, a)
            put(fs, hs, a)
            put(m01, [coupling * x for x in c], a)
            fu, fv = get(force, a, 0), get(force, a, 1)
            for k in every:
                along, across = he[k] + hw[k], hn[k] + hs[k]
                base = fr[k] + 0.5
                ru = inside / (4.0 * along + across + base)
                rv = inside / (along + 4.0 * across + base)
                rdu[a, :, lanes(k)] = ru
                rdv[a, :, lanes(k)] = rv
                v1[a, 0, :, lanes(k)] = ru * fu[k]
                v1[a, 1, :, lanes(k)] = rv * fv[k]

        def sweep(src, dst):
            def body(a):
                he, hw, hn, hs, m = get(fe, a), get(fw, a), get(fn, a), get(fs, a), get(m01, a)
                un, uc, us = get(src, a - 1, 0), get(src, a, 0), get(src, a + 1, 0)
                vn, vc, vs = get(src, a - 1, 1), get(src, a, 1), get(src, a + 1, 1)
                ue, uw, ve, vw = east(uc), west(uc), east(vc), west(vc)
                xu, xv = cross(un, us), cross(vn, vs)
                for k in every:
                    lat_u = he[k] * ue[k] + hw[k] * uw[k]
                    ver_u = hn[k] * un[k] + hs[k] * us[k]
                    lat_v = he[k] * ve[k] + hw[k] * vw[k]
                    ver_v = hn[k] * vn[k] + hs[k] * vs[k]
                    off_u = 4.0 * lat_u + ver_u + m[k] * xv[k]
                    off_v = lat_v + 4.0 * ver_v + m[k] * xu[k]
                    at = (slice(None), lanes(k))
                    dst[(a, 0, *at)] = keep * uc[k] + v1[(a, 0, *at)] + rdu[(a, *at)] * off_u
                    dst[(a, 1, *at)] = keep * vc[k] + v1[(a, 1, *at)] + rdv[(a, *at)] * off_v

            return body

        rows(1, ROWS - 1, coefficients)
        rows(2, ROWS - 2, sweep(v1, v2))
        rows(3, ROWS - 3, sweep(v2, v3))

        for copy in halo:
            copy.wait_recv()
        for k in every:
            stiff[OFF - 1, :, lanes(k)] = stiff[OFF - 1, :, lanes(k)] * has_up
            stiff[OFF + ROWS, :, lanes(k)] = stiff[OFF + ROWS, :, lanes(k)] * has_down
        rows(-3, 1, coefficients)
        rows(ROWS - 1, ROWS + 3, coefficients)
        for a in (0, HELD - 1):
            put(m01, [coupling * x for x in get(stiff, a)], a)
        rows(-2, 2, sweep(v1, v2))
        rows(ROWS - 2, ROWS + 2, sweep(v1, v2))
        rows(-1, 3, sweep(v2, v3))
        rows(ROWS - 3, ROWS + 1, sweep(v2, v3))
        rows(0, ROWS, sweep(v3, v4))

        loads[4].wait()

        def last_adjoint(a):
            m = get(m01, a)
            for comp, rd in ((0, rdu), (1, rdv)):
                lam = [x - y for x, y in zip(get(v4, a, comp), raw(oraw, a - OFF, comp))]
                p = [r * x for r, x in zip(get(rd, a), lam)]
                put(l4, lam, a, comp)
                put(p4, p, a, comp)
                put(q4, [x * y for x, y in zip(m, p)], a, comp)

        rows(0, ROWS, last_adjoint)
        back = [
            send(l4.at[pl.ds(OFF, 3)], l4.at[pl.ds(OFF + ROWS, 3)], asend.at[0], arecv.at[0], {"row": up}),
            send(l4.at[pl.ds(OFF + ROWS - 3, 3)], l4.at[pl.ds(OFF - 3, 3)], asend.at[1], arecv.at[1], {"row": down}),
            send(p4.at[pl.ds(OFF + 3, 1)], p4.at[pl.ds(OFF + ROWS + 3, 1)], asend.at[2], arecv.at[2], {"row": up}),
            send(p4.at[pl.ds(OFF + ROWS - 4, 1)], p4.at[pl.ds(0, 1)], asend.at[3], arecv.at[3], {"row": down}),
        ]

        def terms(a, p, before, after):
            pu, pv = get(p, a, 0), get(p, a, 1)
            un, uc, us = get(before, a - 1, 0), get(before, a, 0), get(before, a + 1, 0)
            vn, vc, vs = get(before, a - 1, 1), get(before, a, 1), get(before, a + 1, 1)
            ue, uw, ve, vw = east(uc), west(uc), east(vc), west(vc)
            xu, xv = cross(un, us), cross(vn, vs)
            au, av = get(after, a, 0), get(after, a, 1)
            out = []
            for k in every:
                pu4, pv4 = 4.0 * pu[k], 4.0 * pv[k]
                out.append((
                    pu[k] * un[k] + pv4 * vn[k],
                    pu[k] * us[k] + pv4 * vs[k],
                    pu4 * ue[k] + pv[k] * ve[k],
                    pu4 * uw[k] + pv[k] * vw[k],
                    pu[k] * xv[k] + pv[k] * xu[k],
                    pu[k] * (au[k] - keep * uc[k]),
                    pv[k] * (av[k] - keep * vc[k]),
                ))
            return out

        held = (accn, accs, acce, accw, accc, accu, accv)

        def last_terms(a):
            for k, values in enumerate(terms(a, p4, v3, v4)):
                for ref, value in zip(held, values):
                    ref[a, :, lanes(k)] = value

        rows(0, ROWS, last_terms)
        inv = 1.0 / relax
        for k in every:
            for slot, (a, ref) in enumerate(((OFF, accn), (OFF + ROWS - 1, accs))):
                at = (a, slice(None), lanes(k))
                g4out[slot, :, lanes(k)] = ref[at] - inv * (accu[at] + 4.0 * accv[at])
            for a in (OFF - 1, OFF + ROWS):
                for ref in held:
                    ref[a, :, lanes(k)] = zero
        back.append(send(g4out.at[0], g4in.at[1], asend.at[4], arecv.at[4], {"row": up}))
        back.append(send(g4out.at[1], g4in.at[0], asend.at[5], arecv.at[5], {"row": down}))

        def adjoint_row(a, lam, p, q):
            he, hw, hn, hs = get(fe, a), get(fw, a), get(fn, a), get(fs, a)
            result = []
            for comp, (along, across) in enumerate(((4.0, 1.0), (1.0, 4.0))):
                pn, pc, ps = get(p, a - 1, comp), get(p, a, comp), get(p, a + 1, comp)
                pe, pw = east(pc), west(pc)
                x = cross(get(q, a - 1, 1 - comp), get(q, a + 1, 1 - comp))
                la = get(lam, a, comp)
                new = []
                for k in every:
                    lat = he[k] * pe[k] + hw[k] * pw[k]
                    ver = hn[k] * pn[k] + hs[k] * ps[k]
                    lat = 4.0 * lat if comp == 0 else lat
                    ver = 4.0 * ver if comp == 1 else ver
                    new.append(keep * la[k] + lat + ver + x[k])
                result.append(new)
            return result

        def adjoint(lam, p, q, lam_to, p_to, q_to):
            def body(a):
                m = get(m01, a)
                for comp, (new, rd) in enumerate(zip(adjoint_row(a, lam, p, q), (rdu, rdv))):
                    pp = [r * x for r, x in zip(get(rd, a), new)]
                    put(lam_to, new, a, comp)
                    put(p_to, pp, a, comp)
                    put(q_to, [x * y for x, y in zip(m, pp)], a, comp)

            return body

        third = adjoint(l4, p4, q4, l3, p3, q3)
        second = adjoint(l3, p3, q3, l2, p2, q2)

        def finish(a):
            t3, t2 = terms(a, p3, v2, v3), terms(a, p2, v1, v2)
            l1 = adjoint_row(a, l2, p2, q2)
            east_part, west_part, rest = [], [], []
            for k in every:
                at = (a, slice(None), lanes(k))
                tn, ts, te, tw, tc, tu, tv = (
                    ref[at] + x + y for ref, x, y in zip(held, t3[k], t2[k])
                )
                tu = inv * (tu + rdu[at] * l1[0][k] * v1[(a, 0, *at[1:])])
                tv = inv * (tv + rdv[at] * l1[1][k] * v1[(a, 1, *at[1:])])
                wide, tall = 4.0 * tu + tv, tu + 4.0 * tv
                tn, ts, te, tw = tn - tall, ts - tall, te - wide, tw - wide
                facen[at] = tn
                faces[at] = ts
                accu[at] = tu + tv
                east_part.append(te)
                west_part.append(tw)
                rest.append(tn + ts + te + tw + (2.0 * coupling) * tc)
            moved = zip(rest, east(west_part), west(east_part))
            put(own, [0.5 * (r + x + y) for r, x, y in moved], a)

        rows(1, ROWS - 1, third)
        rows(2, ROWS - 2, second)
        rows(3, ROWS - 3, finish)

        for copy in back:
            copy.wait_recv()

        def edge_adjoint(a):
            m = get(m01, a)
            for comp, rd in ((0, rdu), (1, rdv)):
                p = [r * x for r, x in zip(get(rd, a), get(l4, a, comp))]
                put(p4, p, a, comp)
                put(q4, [x * y for x, y in zip(m, p)], a, comp)

        rows(-3, 0, edge_adjoint)
        rows(ROWS, ROWS + 3, edge_adjoint)
        for a in (0, HELD - 1):
            for comp in (0, 1):
                put(q4, [x * y for x, y in zip(get(m01, a), get(p4, a, comp))], a, comp)
        rows(-3, 1, third)
        rows(ROWS - 1, ROWS + 3, third)
        rows(-2, 2, second)
        rows(ROWS - 2, ROWS + 2, second)
        rows(-1, 3, finish)
        rows(ROWS - 3, ROWS + 1, finish)
        for k in every:
            at = (OFF - 1, slice(None), lanes(k))
            faces[at] = faces[at] + has_up * g4in[0, :, lanes(k)]
            at = (OFF + ROWS, slice(None), lanes(k))
            facen[at] = facen[at] + has_down * g4in[1, :, lanes(k)]

        def gradients(a):
            i = a - OFF
            for k in every:
                at = (slice(None), lanes(k))
                grad[(i, *at)] = -fric[(a, *at)] * accu[(a, *at)]
                both = own[(a, *at)] + 0.5 * (faces[(a - 1, *at)] + facen[(a + 1, *at)])
                grad[(i + ROWS, *at)] = stiff[(a, *at)] * both

        rows(0, ROWS, gradients)

        order = list(reversed(range(len(peers))))
        scatter = [
            send(grad.at[peers[k]], rsbuf.at[k], rsend.at[k], rrecv.at[k], {"epoch": peers[k]})
            for k in order
        ]
        mine = get(grad, ep)
        for copy, k in zip(scatter, order):
            copy.wait_recv()
            mine = [x + y for x, y in zip(mine, get(rsbuf, k))]
        put(total, mine, ep)
        put(summed, mine)
        sq = mine[0] * mine[0]
        for k in range(1, pieces):
            sq = sq + mine[k] * mine[k]
        sq = jnp.sum(sq, axis=0, keepdims=True)
        sqout[...] = sq
        sqin[ep] = sq

        squares = [
            send(sqout, sqin.at[ep], ssend.at[k], srecv.at[k], {"epoch": peers[k]}) for k in order
        ]
        gather = [
            send(summed, total.at[ep], gsend.at[k], grecv.at[k], {"epoch": peers[k]}) for k in order
        ]
        for copy in squares:
            copy.wait_recv()
        tot_q, tot_r = sqin[0], sqin[n_epoch // 2]
        for k in range(1, n_epoch // 2):
            tot_q = tot_q + sqin[k]
            tot_r = tot_r + sqin[n_epoch // 2 + k]
        rowout[0] = tot_q
        rowout[1] = tot_r
        across = [
            send(rowout, rowin.at[k - 1], tsend.at[k - 1], trecv.at[k - 1], {"row": lax.rem(me + k, n_row)})
            for k in range(1, n_row)
        ]
        for k, copy in enumerate(across):
            copy.wait_recv()
            tot_q = tot_q + rowin[k, 0]
            tot_r = tot_r + rowin[k, 1]
        factors = []
        for tot in (tot_q, tot_r):
            mean = jnp.sum(tot, axis=1, keepdims=True) / cells
            factor = step_size / jnp.sqrt(mean + 1e-6)
            factors.append(jnp.broadcast_to(factor, (SUB, LANE)))
        for copy in gather:
            copy.wait_recv()

        def update(a):
            i = a - OFF
            for ref, old, shift, factor in (
                (outq, lfraw, 0, factors[0]), (outr, lrraw, ROWS, factors[1])
            ):
                g = get(total, i + shift)
                for k in every:
                    at = (pl.ds(k * SUB + i, SUB, stride=span), slice(None))
                    ref[at] = old[at] - factor * g[k]

        rows(0, ROWS, update)

        for copy in halo + back + scatter + squares + gather + across:
            copy.wait_send()

    return kernel


def tiles(x):
    lead = x.shape[:-2]
    x = x.reshape(*lead, ROWS, x.shape[-1] // LANE, LANE)
    return jnp.swapaxes(x, -2, -3).reshape(-1, LANE)


def solution(mesh):
    n_epoch, n_row = mesh.shape["epoch"], mesh.shape["row"]

    def on_device(forcing, observed, log_friction, log_rheology, grounded):
        cols = forcing.shape[-1]
        width = cols // SUB
        raw_rows = ROWS * cols // LANE
        row = pltpu.VMEM((HELD, SUB, width), jnp.float32)
        pair = pltpu.VMEM((HELD, 2, SUB, width), jnp.float32)
        plain = lambda *lead: pltpu.VMEM((*lead, SUB, width), jnp.float32)
        dma = lambda n: pltpu.SemaphoreType.DMA((n,))
        scratch = [
            pltpu.VMEM((2 * raw_rows, LANE), jnp.float32),
            pltpu.VMEM((2 * raw_rows, LANE), jnp.float32),
            pltpu.VMEM((raw_rows, LANE), jnp.float32),
            pltpu.VMEM((raw_rows, LANE), jnp.float32),
            pltpu.VMEM((raw_rows, LANE), jnp.int32),
            row, row, pair, row, row, row, row, row, row, row,
            pair, pair, pair, pair,
            *([pair] * 9),
            *([row] * 7),
            row, row, row, plain(n_epoch), plain(2), plain(2),
            plain(n_epoch - 1), plain(), plain(n_epoch),
            pltpu.VMEM((1, LANE), jnp.float32),
            pltpu.VMEM((n_epoch, 1, LANE), jnp.float32),
            pltpu.VMEM((2, 1, LANE), jnp.float32),
            pltpu.VMEM((n_row - 1, 2, 1, LANE), jnp.float32),
            dma(5), dma(6), dma(6), dma(6), dma(6),
            *([dma(n_epoch - 1)] * 6),
            *([dma(n_row - 1)] * 2),
        ]
        shape = jax.ShapeDtypeStruct((raw_rows, LANE), jnp.float32)
        outs = pl.pallas_call(
            make_kernel(n_epoch, n_row, cols),
            out_shape=(shape, shape),
            in_specs=[pl.BlockSpec(memory_space=pl.ANY)] * 5,
            out_specs=(pl.BlockSpec(memory_space=pltpu.VMEM),) * 2,
            scratch_shapes=scratch,
            compiler_params=pltpu.CompilerParams(
                collective_id=0, has_side_effects=True, vmem_limit_bytes=60 * 2**20
            ),
            name="inversion_step",
        )(*(tiles(x) for x in (forcing, observed, log_friction, log_rheology, grounded)))

        def whole(x):
            return jnp.swapaxes(x.reshape(cols // LANE, ROWS, LANE), 0, 1).reshape(ROWS, cols)

        return whole(outs[0]), whole(outs[1])

    in_specs = (
        P("epoch", None, "row", None),
        P("epoch", None, "row", None),
        P("row", None),
        P("row", None),
        P("row", None),
    )
    out_specs = (P("row", None), P("row", None))
    return jax.shard_map(
        on_device, mesh=mesh, in_specs=in_specs, out_specs=out_specs, check_vma=False
    )
```

```python
import math

import jax
import jax.numpy as jnp
from jax import lax
from jax.experimental import pallas as pl
from jax.experimental.pallas import tpu as pltpu
from jax.sharding import PartitionSpec as P

relax = 0.9
coupling = 0.1
step_size = 0.5
keep = 1.0 - relax

MESH = pl.DeviceIdType.MESH
ROWS = 8
OFF = 4
HELD = ROWS + 2 * OFF
SUB, LANE = 8, 128


def make_kernel(n_epoch, n_row, cols):
    pieces = cols // (SUB * LANE)
    span = pieces * SUB
    side = math.isqrt(n_epoch)
    split = n_epoch // ROWS
    width = pieces // split
    cells = n_row * ROWS * cols

    def kernel(
        f_in, o_in, lf_in, lr_in, gr_in, outq, outr,
        fraw, oraw, lfraw, lrraw, grraw,
        stiff, fric, force, fe, fw, fn, fs, m01, rdu, rdv,
        v1, v2, v3, v4,
        l4, p4, q4, l3, p3, q3, l2, p2, q2,
        accn, accs, acce, accw, accc, accu, accv,
        facen, faces, own, grad, g4out, g4in,
        rsbuf, mid, lastbuf, total, sqout, sqin, rowout, rowin,
        load_sem, hsend, hrecv, asend, arecv, rsend, rrecv, gsend, grecv, ssend, srecv, tsend, trecv,
    ):
        me = lax.axis_index("row")
        ep = lax.axis_index("epoch")
        up = lax.rem(me + n_row - 1, n_row)
        down = lax.rem(me + 1, n_row)
        has_up = (me > 0).astype(jnp.float32)
        has_down = (me < n_row - 1).astype(jnp.float32)

        loads = [
            pltpu.make_async_copy(src, dst, load_sem.at[k])
            for k, (src, dst) in enumerate(
                ((lr_in, lrraw), (lf_in, lfraw), (gr_in, grraw), (f_in, fraw), (o_in, oraw))
            )
        ]
        for load in loads:
            load.start()

        ex, ey = ep // side, lax.rem(ep, side)
        peers = []
        for dx in range(side):
            for dy in range(side):
                if dx or dy:
                    peers.append(lax.rem(ex + dx, side) * side + lax.rem(ey + dy, side))

        barrier = pltpu.get_barrier_semaphore()
        for k in range(1, n_row):
            pl.semaphore_signal(
                barrier, inc=1, device_id={"row": lax.rem(me + k, n_row)}, device_id_type=MESH
            )
        for peer in peers:
            pl.semaphore_signal(barrier, inc=1, device_id={"epoch": peer}, device_id_type=MESH)

        lane = lax.broadcasted_iota(jnp.int32, (SUB, LANE), 1)
        sub = lax.broadcasted_iota(jnp.int32, (SUB, LANE), 0)
        last_lane, first_lane = lane == LANE - 1, lane == 0
        last_sub, first_sub = sub == SUB - 1, sub == 0
        zero = jnp.zeros((SUB, LANE), jnp.float32)
        every = range(pieces)

        def east(x):
            r = [pltpu.roll(p, LANE - 1, 1) for p in x]
            end = jnp.where(last_sub, zero, pltpu.roll(r[0], SUB - 1, 0))
            return [jnp.where(last_lane, r[k + 1] if k + 1 < pieces else end, r[k]) for k in every]

        def west(x):
            r = [pltpu.roll(p, 1, 1) for p in x]
            end = jnp.where(first_sub, zero, pltpu.roll(r[-1], 1, 0))
            return [jnp.where(first_lane, r[k - 1] if k else end, r[k]) for k in every]

        def lanes(k):
            return slice(k * LANE, (k + 1) * LANE)

        def get(ref, *at):
            return [ref[(*at, slice(None), lanes(k))] for k in every]

        def put(ref, x, *at):
            for k in every:
                ref[(*at, slice(None), lanes(k))] = x[k]

        def raw(ref, i, part=0):
            return [ref[pl.ds(part * span * SUB + k * SUB + i, SUB, stride=span), :] for k in every]

        def cross(north, south):
            d = [s - n for s, n in zip(south, north)]
            return [a - b for a, b in zip(east(d), west(d))]

        def rows(lo, hi, body):
            def step(a, carry):
                body(a)
                return carry

            lax.fori_loop(lo + OFF, hi + OFF, step, 0)

        loads[0].wait()

        def own_stiff(a):
            put(stiff, [jnp.exp(x) for x in raw(lrraw, a - OFF)], a)

        rows(0, ROWS, own_stiff)
        loads[1].wait()
        loads[2].wait()

        def own_fric(a):
            held_up = zip(raw(grraw, a - OFF), raw(lfraw, a - OFF))
            put(fric, [g.astype(jnp.float32) * jnp.exp(x) for g, x in held_up], a)

        rows(0, ROWS, own_fric)
        loads[3].wait()

        def own_force(a):
            put(force, raw(fraw, a - OFF, 0), a, 0)
            put(force, raw(fraw, a - OFF, 1), a, 1)

        rows(0, ROWS, own_force)

        pl.semaphore_wait(barrier, n_row - 1 + len(peers))

        def send(src, dst, ssem, rsem, where):
            copy = pltpu.make_async_remote_copy(
                src_ref=src, dst_ref=dst, send_sem=ssem, recv_sem=rsem,
                device_id=where, device_id_type=MESH,
            )
            copy.start()
            return copy

        halo = []
        for k, (ref, depth) in enumerate(((stiff, 4), (fric, 3), (force, 3))):
            halo.append(send(
                ref.at[pl.ds(OFF, depth)], ref.at[pl.ds(OFF + ROWS, depth)],
                hsend.at[2 * k], hrecv.at[2 * k], {"row": up},
            ))
            halo.append(send(
                ref.at[pl.ds(OFF + ROWS - depth, depth)], ref.at[pl.ds(OFF - depth, depth)],
                hsend.at[2 * k + 1], hrecv.at[2 * k + 1], {"row": down},
            ))

        def coefficients(a):
            c, n, s = get(stiff, a), get(stiff, a - 1), get(stiff, a + 1)
            he = [0.5 * (x + y) for x, y in zip(c, east(c))]
            hw = [0.5 * (x + y) for x, y in zip(c, west(c))]
            hn = [0.5 * (x + y) for x, y in zip(c, n)]
            hs = [0.5 * (x + y) for x, y in zip(c, s)]
            fr = get(fric, a)
            inside = relax * jnp.where(a < OFF, has_up, jnp.where(a >= OFF + ROWS, has_down, 1.0))
            put(fe, he, a)
            put(fw, hw, a)
            put(fn, hn, a)
            put(fs, hs, a)
            put(m01, [coupling * x for x in c], a)
            fu, fv = get(force, a, 0), get(force, a, 1)
            for k in every:
                along, across = he[k] + hw[k], hn[k] + hs[k]
                base = fr[k] + 0.5
                ru = inside / (4.0 * along + across + base)
                rv = inside / (along + 4.0 * across + base)
                rdu[a, :, lanes(k)] = ru
                rdv[a, :, lanes(k)] = rv
                v1[a, 0, :, lanes(k)] = ru * fu[k]
                v1[a, 1, :, lanes(k)] = rv * fv[k]

        def sweep(src, dst):
            def body(a):
                he, hw, hn, hs, m = get(fe, a), get(fw, a), get(fn, a), get(fs, a), get(m01, a)
                un, uc, us = get(src, a - 1, 0), get(src, a, 0), get(src, a + 1, 0)
                vn, vc, vs = get(src, a - 1, 1), get(src, a, 1), get(src, a + 1, 1)
                ue, uw, ve, vw = east(uc), west(uc), east(vc), west(vc)
                xu, xv = cross(un, us), cross(vn, vs)
                for k in every:
                    lat_u = he[k] * ue[k] + hw[k] * uw[k]
                    ver_u = hn[k] * un[k] + hs[k] * us[k]
                    lat_v = he[k] * ve[k] + hw[k] * vw[k]
                    ver_v = hn[k] * vn[k] + hs[k] * vs[k]
                    off_u = 4.0 * lat_u + ver_u + m[k] * xv[k]
                    off_v = lat_v + 4.0 * ver_v + m[k] * xu[k]
                    at = (slice(None), lanes(k))
                    dst[(a, 0, *at)] = keep * uc[k] + v1[(a, 0, *at)] + rdu[(a, *at)] * off_u
                    dst[(a, 1, *at)] = keep * vc[k] + v1[(a, 1, *at)] + rdv[(a, *at)] * off_v

            return body

        rows(1, ROWS - 1, coefficients)
        rows(2, ROWS - 2, sweep(v1, v2))
        rows(3, ROWS - 3, sweep(v2, v3))

        for copy in halo:
            copy.wait_recv()
        for k in every:
            stiff[OFF - 1, :, lanes(k)] = stiff[OFF - 1, :, lanes(k)] * has_up
            stiff[OFF + ROWS, :, lanes(k)] = stiff[OFF + ROWS, :, lanes(k)] * has_down
        rows(-3, 1, coefficients)
        rows(ROWS - 1, ROWS + 3, coefficients)
        for a in (0, HELD - 1):
            put(m01, [coupling * x for x in get(stiff, a)], a)
        rows(-2, 2, sweep(v1, v2))
        rows(ROWS - 2, ROWS + 2, sweep(v1, v2))
        rows(-1, 3, sweep(v2, v3))
        rows(ROWS - 3, ROWS + 1, sweep(v2, v3))
        rows(0, ROWS, sweep(v3, v4))

        loads[4].wait()

        def last_adjoint(a):
            m = get(m01, a)
            for comp, rd in ((0, rdu), (1, rdv)):
                lam = [x - y for x, y in zip(get(v4, a, comp), raw(oraw, a - OFF, comp))]
                p = [r * x for r, x in zip(get(rd, a), lam)]
                put(l4, lam, a, comp)
                put(p4, p, a, comp)
                put(q4, [x * y for x, y in zip(m, p)], a, comp)

        rows(0, ROWS, last_adjoint)
        back = [
            send(l4.at[pl.ds(OFF, 3)], l4.at[pl.ds(OFF + ROWS, 3)], asend.at[0], arecv.at[0], {"row": up}),
            send(l4.at[pl.ds(OFF + ROWS - 3, 3)], l4.at[pl.ds(OFF - 3, 3)], asend.at[1], arecv.at[1], {"row": down}),
            send(p4.at[pl.ds(OFF + 3, 1)], p4.at[pl.ds(OFF + ROWS + 3, 1)], asend.at[2], arecv.at[2], {"row": up}),
            send(p4.at[pl.ds(OFF + ROWS - 4, 1)], p4.at[pl.ds(0, 1)], asend.at[3], arecv.at[3], {"row": down}),
        ]

        def terms(a, p, before, after):
            pu, pv = get(p, a, 0), get(p, a, 1)
            un, uc, us = get(before, a - 1, 0), get(before, a, 0), get(before, a + 1, 0)
            vn, vc, vs = get(before, a - 1, 1), get(before, a, 1), get(before, a + 1, 1)
            ue, uw, ve, vw = east(uc), west(uc), east(vc), west(vc)
            xu, xv = cross(un, us), cross(vn, vs)
            au, av = get(after, a, 0), get(after, a, 1)
            out = []
            for k in every:
                pu4, pv4 = 4.0 * pu[k], 4.0 * pv[k]
                out.append((
                    pu[k] * un[k] + pv4 * vn[k],
                    pu[k] * us[k] + pv4 * vs[k],
                    pu4 * ue[k] + pv[k] * ve[k],
                    pu4 * uw[k] + pv[k] * vw[k],
                    pu[k] * xv[k] + pv[k] * xu[k],
                    pu[k] * (au[k] - keep * uc[k]),
                    pv[k] * (av[k] - keep * vc[k]),
                ))
            return out

        held = (accn, accs, acce, accw, accc, accu, accv)

        def last_terms(a):
            for k, values in enumerate(terms(a, p4, v3, v4)):
                for ref, value in zip(held, values):
                    ref[a, :, lanes(k)] = value

        rows(0, ROWS, last_terms)
        inv = 1.0 / relax
        for k in every:
            for slot, (a, ref) in enumerate(((OFF, accn), (OFF + ROWS - 1, accs))):
                at = (a, slice(None), lanes(k))
                g4out[slot, :, lanes(k)] = ref[at] - inv * (accu[at] + 4.0 * accv[at])
            for a in (OFF - 1, OFF + ROWS):
                for ref in held:
                    ref[a, :, lanes(k)] = zero
        back.append(send(g4out.at[0], g4in.at[1], asend.at[4], arecv.at[4], {"row": up}))
        back.append(send(g4out.at[1], g4in.at[0], asend.at[5], arecv.at[5], {"row": down}))

        def adjoint_row(a, lam, p, q):
            he, hw, hn, hs = get(fe, a), get(fw, a), get(fn, a), get(fs, a)
            result = []
            for comp, (along, across) in enumerate(((4.0, 1.0), (1.0, 4.0))):
                pn, pc, ps = get(p, a - 1, comp), get(p, a, comp), get(p, a + 1, comp)
                pe, pw = east(pc), west(pc)
                x = cross(get(q, a - 1, 1 - comp), get(q, a + 1, 1 - comp))
                la = get(lam, a, comp)
                new = []
                for k in every:
                    lat = he[k] * pe[k] + hw[k] * pw[k]
                    ver = hn[k] * pn[k] + hs[k] * ps[k]
                    lat = 4.0 * lat if comp == 0 else lat
                    ver = 4.0 * ver if comp == 1 else ver
                    new.append(keep * la[k] + lat + ver + x[k])
                result.append(new)
            return result

        def adjoint(lam, p, q, lam_to, p_to, q_to):
            def body(a):
                m = get(m01, a)
                for comp, (new, rd) in enumerate(zip(adjoint_row(a, lam, p, q), (rdu, rdv))):
                    pp = [r * x for r, x in zip(get(rd, a), new)]
                    put(lam_to, new, a, comp)
                    put(p_to, pp, a, comp)
                    put(q_to, [x * y for x, y in zip(m, pp)], a, comp)

            return body

        third = adjoint(l4, p4, q4, l3, p3, q3)
        second = adjoint(l3, p3, q3, l2, p2, q2)

        def finish(a):
            t3, t2 = terms(a, p3, v2, v3), terms(a, p2, v1, v2)
            l1 = adjoint_row(a, l2, p2, q2)
            east_part, west_part, rest = [], [], []
            for k in every:
                at = (a, slice(None), lanes(k))
                tn, ts, te, tw, tc, tu, tv = (
                    ref[at] + x + y for ref, x, y in zip(held, t3[k], t2[k])
                )
                tu = inv * (tu + rdu[at] * l1[0][k] * v1[(a, 0, *at[1:])])
                tv = inv * (tv + rdv[at] * l1[1][k] * v1[(a, 1, *at[1:])])
                wide, tall = 4.0 * tu + tv, tu + 4.0 * tv
                tn, ts, te, tw = tn - tall, ts - tall, te - wide, tw - wide
                facen[at] = tn
                faces[at] = ts
                accu[at] = tu + tv
                east_part.append(te)
                west_part.append(tw)
                rest.append(tn + ts + te + tw + (2.0 * coupling) * tc)
            moved = zip(rest, east(west_part), west(east_part))
            put(own, [0.5 * (r + x + y) for r, x, y in moved], a)

        rows(1, ROWS - 1, third)
        rows(2, ROWS - 2, second)
        rows(3, ROWS - 3, finish)

        for copy in back:
            copy.wait_recv()

        def edge_adjoint(a):
            m = get(m01, a)
            for comp, rd in ((0, rdu), (1, rdv)):
                p = [r * x for r, x in zip(get(rd, a), get(l4, a, comp))]
                put(p4, p, a, comp)
                put(q4, [x * y for x, y in zip(m, p)], a, comp)

        rows(-3, 0, edge_adjoint)
        rows(ROWS, ROWS + 3, edge_adjoint)
        for a in (0, HELD - 1):
            for comp in (0, 1):
                put(q4, [x * y for x, y in zip(get(m01, a), get(p4, a, comp))], a, comp)
        def gradients(a):
            for k in every:
                at = (slice(None), lanes(k))
                to = (split * (a - OFF) + k // width, slice(None), lanes(k % width))
                grad[(0, *to)] = -fric[(a, *at)] * accu[(a, *at)]
                both = own[(a, *at)] + 0.5 * (faces[(a - 1, *at)] + facen[(a + 1, *at)])
                grad[(1, *to)] = stiff[(a, *at)] * both

        here = (ex, ey)

        def along(axis, k):
            j = lax.rem(here[axis] + k, side)
            return j, {"epoch": j * side + ey if axis == 0 else ex * side + j}

        def first(f, k):
            j, where = along(f, k)
            n = f * (side - 1) + k - 1
            return j, pltpu.make_async_remote_copy(
                src_ref=grad.at[f, pl.ds(j * side, side)], dst_ref=rsbuf.at[f, k - 1],
                send_sem=rsend.at[n], recv_sem=rrecv.at[n], device_id=where, device_id_type=MESH,
            )

        others = range(1, side)

        def first_sends(low):
            for k in others:
                for f in (0, 1):
                    j, copy = first(f, k)
                    pl.when((j < side // 2) if low else (j >= side // 2))(copy.start)

        rows(-3, 1, third)
        rows(-2, 2, second)
        rows(-1, 3, finish)
        for k in every:
            at = (OFF - 1, slice(None), lanes(k))
            faces[at] = faces[at] + has_up * g4in[0, :, lanes(k)]
        rows(0, ROWS // 2, gradients)
        first_sends(True)

        rows(ROWS - 1, ROWS + 3, third)
        rows(ROWS - 2, ROWS + 2, second)
        rows(ROWS - 3, ROWS + 1, finish)
        for k in every:
            at = (OFF + ROWS, slice(None), lanes(k))
            facen[at] = facen[at] + has_down * g4in[1, :, lanes(k)]
        rows(ROWS // 2, ROWS, gradients)
        first_sends(False)

        scatter = [first(f, k)[1] for k in others for f in (0, 1)]
        for copy in scatter:
            copy.wait_recv()
        cut = [slice(k * LANE, (k + 1) * LANE) for k in range(width)]
        for f in (0, 1):
            for j in range(side):
                for c in cut:
                    x = grad[f, here[f] * side + j, :, c]
                    for k in others:
                        x = x + rsbuf[f, k - 1, j, :, c]
                    mid[f, j, :, c] = x
        for k in others:
            for f in (0, 1):
                j, where = along(1 - f, k)
                n = (2 + f) * (side - 1) + k - 1
                scatter.append(send(mid.at[f, j], lastbuf.at[f, k - 1], rsend.at[n], rrecv.at[n], where))
        for copy in scatter[2 * (side - 1):]:
            copy.wait_recv()
        for f in (0, 1):
            sq = jnp.zeros((SUB, LANE), jnp.float32)
            for c in cut:
                x = mid[f, here[1 - f], :, c]
                for k in others:
                    x = x + lastbuf[f, k - 1, :, c]
                total[f, here[f] * side + here[1 - f], :, c] = x
                sq = sq + x * x
            sq = jnp.sum(sq, axis=0, keepdims=True)
            sqout[f] = sq
            sqin[ep, f] = sq

        order = list(reversed(range(len(peers))))
        squares = [
            send(sqout, sqin.at[ep], ssend.at[k], srecv.at[k], {"epoch": peers[k]}) for k in order
        ]

        gather, onward = [], []

        def share(f, axis, source, slot, copies):
            part = total.at[f, here[f] * side + source]
            for k in others:
                n = (slot * 2 + f) * (side - 1) + k - 1
                copies.append(send(part, part, gsend.at[n], grecv.at[n], along(axis, k)[1]))

        for f in (0, 1):
            share(f, 1 - f, here[1 - f], 0, gather)
        for f in (0, 1):
            share(f, f, here[1 - f], 1, onward)
        for k in others:
            for f in (0, 1):
                gather[f * (side - 1) + k - 1].wait_recv()
                share(f, f, lax.rem(here[1 - f] + side - k, side), 1 + k, onward)
        gather = gather + onward

        for copy in squares:
            copy.wait_recv()
        tot_q, tot_r = sqin[0, 0], sqin[0, 1]
        for k in range(1, n_epoch):
            tot_q = tot_q + sqin[k, 0]
            tot_r = tot_r + sqin[k, 1]
        rowout[0] = tot_q
        rowout[1] = tot_r
        across = [
            send(rowout, rowin.at[k - 1], tsend.at[k - 1], trecv.at[k - 1], {"row": lax.rem(me + k, n_row)})
            for k in range(1, n_row)
        ]
        for k, copy in enumerate(across):
            copy.wait_recv()
            tot_q = tot_q + rowin[k, 0]
            tot_r = tot_r + rowin[k, 1]
        factors = []
        for tot in (tot_q, tot_r):
            mean = jnp.sum(tot, axis=1, keepdims=True) / cells
            factor = step_size / jnp.sqrt(mean + 1e-6)
            factors.append(jnp.broadcast_to(factor, (SUB, LANE)))
        for copy in onward:
            copy.wait_recv()

        def update(a):
            i = a - OFF
            for f, (ref, old) in enumerate(((outq, lfraw), (outr, lrraw))):
                for k in every:
                    at = (pl.ds(k * SUB + i, SUB, stride=span), slice(None))
                    g = total[f, split * i + k // width, :, lanes(k % width)]
                    ref[at] = old[at] - factors[f] * g

        rows(0, ROWS, update)

        for copy in halo + back + scatter + squares + gather + across:
            copy.wait_send()

    return kernel


def tiles(x):
    lead = x.shape[:-2]
    x = x.reshape(*lead, ROWS, x.shape[-1] // LANE, LANE)
    return jnp.swapaxes(x, -2, -3).reshape(-1, LANE)


def solution(mesh):
    n_epoch, n_row = mesh.shape["epoch"], mesh.shape["row"]

    def on_device(forcing, observed, log_friction, log_rheology, grounded):
        cols = forcing.shape[-1]
        width = cols // SUB
        raw_rows = ROWS * cols // LANE
        row = pltpu.VMEM((HELD, SUB, width), jnp.float32)
        pair = pltpu.VMEM((HELD, 2, SUB, width), jnp.float32)
        plain = lambda *lead: pltpu.VMEM((*lead, SUB, width), jnp.float32)
        side = math.isqrt(n_epoch)
        part = lambda *lead: pltpu.VMEM((*lead, SUB, width * ROWS // n_epoch), jnp.float32)
        dma = lambda n: pltpu.SemaphoreType.DMA((n,))
        scratch = [
            pltpu.VMEM((2 * raw_rows, LANE), jnp.float32),
            pltpu.VMEM((2 * raw_rows, LANE), jnp.float32),
            pltpu.VMEM((raw_rows, LANE), jnp.float32),
            pltpu.VMEM((raw_rows, LANE), jnp.float32),
            pltpu.VMEM((raw_rows, LANE), jnp.int32),
            row, row, pair, row, row, row, row, row, row, row,
            pair, pair, pair, pair,
            *([pair] * 9),
            *([row] * 7),
            row, row, row, part(2, n_epoch), plain(2), plain(2),
            part(2, side - 1, side), part(2, side), part(2, side - 1), part(2, n_epoch),
            pltpu.VMEM((2, 1, LANE), jnp.float32),
            pltpu.VMEM((n_epoch, 2, 1, LANE), jnp.float32),
            pltpu.VMEM((2, 1, LANE), jnp.float32),
            pltpu.VMEM((n_row - 1, 2, 1, LANE), jnp.float32),
            dma(5), dma(6), dma(6), dma(6), dma(6),
            *([dma(4 * (side - 1))] * 2),
            *([dma(2 * (side + 1) * (side - 1))] * 2),
            *([dma(n_epoch - 1)] * 2),
            *([dma(n_row - 1)] * 2),
        ]
        shape = jax.ShapeDtypeStruct((raw_rows, LANE), jnp.float32)
        outs = pl.pallas_call(
            make_kernel(n_epoch, n_row, cols),
            out_shape=(shape, shape),
            in_specs=[pl.BlockSpec(memory_space=pl.ANY)] * 5,
            out_specs=(pl.BlockSpec(memory_space=pltpu.VMEM),) * 2,
            scratch_shapes=scratch,
            compiler_params=pltpu.CompilerParams(
                collective_id=0, has_side_effects=True, vmem_limit_bytes=60 * 2**20
            ),
            name="inversion_step",
        )(*(tiles(x) for x in (forcing, observed, log_friction, log_rheology, grounded)))

        def whole(x):
            return jnp.swapaxes(x.reshape(cols // LANE, ROWS, LANE), 0, 1).reshape(ROWS, cols)

        return whole(outs[0]), whole(outs[1])

    in_specs = (
        P("epoch", None, "row", None),
        P("epoch", None, "row", None),
        P("row", None),
        P("row", None),
        P("row", None),
    )
    out_specs = (P("row", None), P("row", None))
    return jax.shard_map(
        on_device, mesh=mesh, in_specs=in_specs, out_specs=out_specs, check_vma=False
    )
```

```python
import math

import jax
import jax.numpy as jnp
from jax import lax
from jax.experimental import pallas as pl
from jax.experimental.pallas import tpu as pltpu
from jax.sharding import PartitionSpec as P

relax = 0.9
coupling = 0.1
step_size = 0.5
keep = 1.0 - relax

MESH = pl.DeviceIdType.MESH
ROWS = 8
OFF = 4
HELD = ROWS + 2 * OFF
SUB, LANE = 8, 128


def make_kernel(n_epoch, n_row, cols):
    pieces = cols // (SUB * LANE)
    span = pieces * SUB
    side = math.isqrt(n_epoch)
    cells = n_row * ROWS * cols

    def kernel(
        f_in, o_in, lf_in, lr_in, gr_in, outq, outr,
        fraw, oraw, lfraw, lrraw, grraw,
        stiff, fric, force, fe, fw, fn, fs, m01, rdu, rdv,
        v1, v2, v3, v4,
        l4, p4, q4, l3, p3, q3, l2, p2, q2,
        accn, accs, acce, accw, accc, accu, accv,
        facen, faces, own, grad, g4out, g4in,
        rsbuf, summed, total, sqout, sqin, rowout, rowin,
        load_sem, hsend, hrecv, asend, arecv, rsend, rrecv, gsend, grecv, ssend, srecv, tsend, trecv,
    ):
        me = lax.axis_index("row")
        ep = lax.axis_index("epoch")
        up = lax.rem(me + n_row - 1, n_row)
        down = lax.rem(me + 1, n_row)
        has_up = (me > 0).astype(jnp.float32)
        has_down = (me < n_row - 1).astype(jnp.float32)

        loads = [
            pltpu.make_async_copy(src, dst, load_sem.at[k])
            for k, (src, dst) in enumerate(
                ((lr_in, lrraw), (lf_in, lfraw), (gr_in, grraw), (f_in, fraw), (o_in, oraw))
            )
        ]
        for load in loads:
            load.start()

        ex, ey = ep // side, lax.rem(ep, side)
        peers = []
        for dx in range(side):
            for dy in range(side):
                if dx or dy:
                    peers.append(lax.rem(ex + dx, side) * side + lax.rem(ey + dy, side))

        barrier = pltpu.get_barrier_semaphore()
        for k in range(1, n_row):
            pl.semaphore_signal(
                barrier, inc=1, device_id={"row": lax.rem(me + k, n_row)}, device_id_type=MESH
            )
        for peer in peers:
            pl.semaphore_signal(barrier, inc=1, device_id={"epoch": peer}, device_id_type=MESH)

        lane = lax.broadcasted_iota(jnp.int32, (SUB, LANE), 1)
        sub = lax.broadcasted_iota(jnp.int32, (SUB, LANE), 0)
        last_lane, first_lane = lane == LANE - 1, lane == 0
        last_sub, first_sub = sub == SUB - 1, sub == 0
        zero = jnp.zeros((SUB, LANE), jnp.float32)
        every = range(pieces)

        def east(x):
            r = [pltpu.roll(p, LANE - 1, 1) for p in x]
            end = jnp.where(last_sub, zero, pltpu.roll(r[0], SUB - 1, 0))
            return [jnp.where(last_lane, r[k + 1] if k + 1 < pieces else end, r[k]) for k in every]

        def west(x):
            r = [pltpu.roll(p, 1, 1) for p in x]
            end = jnp.where(first_sub, zero, pltpu.roll(r[-1], 1, 0))
            return [jnp.where(first_lane, r[k - 1] if k else end, r[k]) for k in every]

        def lanes(k):
            return slice(k * LANE, (k + 1) * LANE)

        def get(ref, *at):
            return [ref[(*at, slice(None), lanes(k))] for k in every]

        def put(ref, x, *at):
            for k in every:
                ref[(*at, slice(None), lanes(k))] = x[k]

        def raw(ref, i, part=0):
            return [ref[pl.ds(part * span * SUB + k * SUB + i, SUB, stride=span), :] for k in every]

        def cross(north, south):
            d = [s - n for s, n in zip(south, north)]
            return [a - b for a, b in zip(east(d), west(d))]

        def rows(lo, hi, body):
            by = 2 if (hi - lo) % 2 == 0 else 1

            def step(n, carry):
                for m in range(by):
                    body(lo + OFF + n * by + m)
                return carry

            lax.fori_loop(0, (hi - lo) // by, step, 0)

        loads[0].wait()

        def own_stiff(a):
            put(stiff, [jnp.exp(x) for x in raw(lrraw, a - OFF)], a)

        rows(0, ROWS, own_stiff)
        loads[1].wait()
        loads[2].wait()

        def own_fric(a):
            held_up = zip(raw(grraw, a - OFF), raw(lfraw, a - OFF))
            put(fric, [g.astype(jnp.float32) * jnp.exp(x) for g, x in held_up], a)

        rows(0, ROWS, own_fric)
        loads[3].wait()

        def own_force(a):
            put(force, raw(fraw, a - OFF, 0), a, 0)
            put(force, raw(fraw, a - OFF, 1), a, 1)

        rows(0, ROWS, own_force)

        pl.semaphore_wait(barrier, n_row - 1 + len(peers))

        def send(src, dst, ssem, rsem, where):
            copy = pltpu.make_async_remote_copy(
                src_ref=src, dst_ref=dst, send_sem=ssem, recv_sem=rsem,
                device_id=where, device_id_type=MESH,
            )
            copy.start()
            return copy

        halo = []
        for k, (ref, depth) in enumerate(((stiff, 4), (fric, 3), (force, 3))):
            halo.append(send(
                ref.at[pl.ds(OFF, depth)], ref.at[pl.ds(OFF + ROWS, depth)],
                hsend.at[2 * k], hrecv.at[2 * k], {"row": up},
            ))
            halo.append(send(
                ref.at[pl.ds(OFF + ROWS - depth, depth)], ref.at[pl.ds(OFF - depth, depth)],
                hsend.at[2 * k + 1], hrecv.at[2 * k + 1], {"row": down},
            ))

        def coefficients(a):
            c, n, s = get(stiff, a), get(stiff, a - 1), get(stiff, a + 1)
            he = [0.5 * (x + y) for x, y in zip(c, east(c))]
            hw = [0.5 * (x + y) for x, y in zip(c, west(c))]
            hn = [0.5 * (x + y) for x, y in zip(c, n)]
            hs = [0.5 * (x + y) for x, y in zip(c, s)]
            fr = get(fric, a)
            inside = relax * jnp.where(a < OFF, has_up, jnp.where(a >= OFF + ROWS, has_down, 1.0))
            put(fe, he, a)
            put(fw, hw, a)
            put(fn, hn, a)
            put(fs, hs, a)
            put(m01, [coupling * x for x in c], a)
            fu, fv = get(force, a, 0), get(force, a, 1)
            for k in every:
                along, across = he[k] + hw[k], hn[k] + hs[k]
                base = fr[k] + 0.5
                ru = inside / (4.0 * along + across + base)
                rv = inside / (along + 4.0 * across + base)
                rdu[a, :, lanes(k)] = ru
                rdv[a, :, lanes(k)] = rv
                v1[a, 0, :, lanes(k)] = ru * fu[k]
                v1[a, 1, :, lanes(k)] = rv * fv[k]

        def sweep(src, dst):
            def body(a):
                he, hw, hn, hs, m = get(fe, a), get(fw, a), get(fn, a), get(fs, a), get(m01, a)
                un, uc, us = get(src, a - 1, 0), get(src, a, 0), get(src, a + 1, 0)
                vn, vc, vs = get(src, a - 1, 1), get(src, a, 1), get(src, a + 1, 1)
                ue, uw, ve, vw = east(uc), west(uc), east(vc), west(vc)
                xu, xv = cross(un, us), cross(vn, vs)
                for k in every:
                    lat_u = he[k] * ue[k] + hw[k] * uw[k]
                    ver_u = hn[k] * un[k] + hs[k] * us[k]
                    lat_v = he[k] * ve[k] + hw[k] * vw[k]
                    ver_v = hn[k] * vn[k] + hs[k] * vs[k]
                    off_u = 4.0 * lat_u + ver_u + m[k] * xv[k]
                    off_v = lat_v + 4.0 * ver_v + m[k] * xu[k]
                    at = (slice(None), lanes(k))
                    dst[(a, 0, *at)] = keep * uc[k] + v1[(a, 0, *at)] + rdu[(a, *at)] * off_u
                    dst[(a, 1, *at)] = keep * vc[k] + v1[(a, 1, *at)] + rdv[(a, *at)] * off_v

            return body

        rows(1, ROWS - 1, coefficients)
        rows(2, ROWS - 2, sweep(v1, v2))
        rows(3, ROWS - 3, sweep(v2, v3))

        for copy in halo:
            copy.wait_recv()
        for k in every:
            stiff[OFF - 1, :, lanes(k)] = stiff[OFF - 1, :, lanes(k)] * has_up
            stiff[OFF + ROWS, :, lanes(k)] = stiff[OFF + ROWS, :, lanes(k)] * has_down
        rows(-3, 1, coefficients)
        rows(ROWS - 1, ROWS + 3, coefficients)
        for a in (0, HELD - 1):
            put(m01, [coupling * x for x in get(stiff, a)], a)
        rows(-2, 2, sweep(v1, v2))
        rows(ROWS - 2, ROWS + 2, sweep(v1, v2))
        rows(-1, 3, sweep(v2, v3))
        rows(ROWS - 3, ROWS + 1, sweep(v2, v3))
        rows(0, ROWS, sweep(v3, v4))

        loads[4].wait()

        def last_adjoint(a):
            m = get(m01, a)
            for comp, rd in ((0, rdu), (1, rdv)):
                lam = [x - y for x, y in zip(get(v4, a, comp), raw(oraw, a - OFF, comp))]
                p = [r * x for r, x in zip(get(rd, a), lam)]
                put(l4, lam, a, comp)
                put(p4, p, a, comp)
                put(q4, [x * y for x, y in zip(m, p)], a, comp)

        rows(0, ROWS, last_adjoint)
        back = [
            send(l4.at[pl.ds(OFF, 3)], l4.at[pl.ds(OFF + ROWS, 3)], asend.at[0], arecv.at[0], {"row": up}),
            send(l4.at[pl.ds(OFF + ROWS - 3, 3)], l4.at[pl.ds(OFF - 3, 3)], asend.at[1], arecv.at[1], {"row": down}),
            send(p4.at[pl.ds(OFF + 3, 1)], p4.at[pl.ds(OFF + ROWS + 3, 1)], asend.at[2], arecv.at[2], {"row": up}),
            send(p4.at[pl.ds(OFF + ROWS - 4, 1)], p4.at[pl.ds(0, 1)], asend.at[3], arecv.at[3], {"row": down}),
        ]

        def terms(a, p, before, after):
            pu, pv = get(p, a, 0), get(p, a, 1)
            un, uc, us = get(before, a - 1, 0), get(before, a, 0), get(before, a + 1, 0)
            vn, vc, vs = get(before, a - 1, 1), get(before, a, 1), get(before, a + 1, 1)
            ue, uw, ve, vw = east(uc), west(uc), east(vc), west(vc)
            xu, xv = cross(un, us), cross(vn, vs)
            au, av = get(after, a, 0), get(after, a, 1)
            out = []
            for k in every:
                pu4, pv4 = 4.0 * pu[k], 4.0 * pv[k]
                out.append((
                    pu[k] * un[k] + pv4 * vn[k],
                    pu[k] * us[k] + pv4 * vs[k],
                    pu4 * ue[k] + pv[k] * ve[k],
                    pu4 * uw[k] + pv[k] * vw[k],
                    pu[k] * xv[k] + pv[k] * xu[k],
                    pu[k] * (au[k] - keep * uc[k]),
                    pv[k] * (av[k] - keep * vc[k]),
                ))
            return out

        held = (accn, accs, acce, accw, accc, accu, accv)

        def last_terms(a):
            for k, values in enumerate(terms(a, p4, v3, v4)):
                for ref, value in zip(held, values):
                    ref[a, :, lanes(k)] = value

        rows(0, ROWS, last_terms)
        inv = 1.0 / relax
        for k in every:
            for slot, (a, ref) in enumerate(((OFF, accn), (OFF + ROWS - 1, accs))):
                at = (a, slice(None), lanes(k))
                g4out[slot, :, lanes(k)] = ref[at] - inv * (accu[at] + 4.0 * accv[at])
            for a in (OFF - 1, OFF + ROWS):
                for ref in held:
                    ref[a, :, lanes(k)] = zero
        back.append(send(g4out.at[0], g4in.at[1], asend.at[4], arecv.at[4], {"row": up}))
        back.append(send(g4out.at[1], g4in.at[0], asend.at[5], arecv.at[5], {"row": down}))

        def adjoint_row(a, lam, p, q):
            he, hw, hn, hs = get(fe, a), get(fw, a), get(fn, a), get(fs, a)
            result = []
            for comp, (along, across) in enumerate(((4.0, 1.0), (1.0, 4.0))):
                pn, pc, ps = get(p, a - 1, comp), get(p, a, comp), get(p, a + 1, comp)
                pe, pw = east(pc), west(pc)
                x = cross(get(q, a - 1, 1 - comp), get(q, a + 1, 1 - comp))
                la = get(lam, a, comp)
                new = []
                for k in every:
                    lat = he[k] * pe[k] + hw[k] * pw[k]
                    ver = hn[k] * pn[k] + hs[k] * ps[k]
                    lat = 4.0 * lat if comp == 0 else lat
                    ver = 4.0 * ver if comp == 1 else ver
                    new.append(keep * la[k] + lat + ver + x[k])
                result.append(new)
            return result

        def adjoint(lam, p, q, lam_to, p_to, q_to):
            def body(a):
                m = get(m01, a)
                for comp, (new, rd) in enumerate(zip(adjoint_row(a, lam, p, q), (rdu, rdv))):
                    pp = [r * x for r, x in zip(get(rd, a), new)]
                    put(lam_to, new, a, comp)
                    put(p_to, pp, a, comp)
                    put(q_to, [x * y for x, y in zip(m, pp)], a, comp)

            return body

        third = adjoint(l4, p4, q4, l3, p3, q3)
        second = adjoint(l3, p3, q3, l2, p2, q2)

        def finish(a):
            t3, t2 = terms(a, p3, v2, v3), terms(a, p2, v1, v2)
            l1 = adjoint_row(a, l2, p2, q2)
            east_part, west_part, rest = [], [], []
            for k in every:
                at = (a, slice(None), lanes(k))
                tn, ts, te, tw, tc, tu, tv = (
                    ref[at] + x + y for ref, x, y in zip(held, t3[k], t2[k])
                )
                tu = inv * (tu + rdu[at] * l1[0][k] * v1[(a, 0, *at[1:])])
                tv = inv * (tv + rdv[at] * l1[1][k] * v1[(a, 1, *at[1:])])
                wide, tall = 4.0 * tu + tv, tu + 4.0 * tv
                tn, ts, te, tw = tn - tall, ts - tall, te - wide, tw - wide
                facen[at] = tn
                faces[at] = ts
                accu[at] = tu + tv
                east_part.append(te)
                west_part.append(tw)
                rest.append(tn + ts + te + tw + (2.0 * coupling) * tc)
            moved = zip(rest, east(west_part), west(east_part))
            put(own, [0.5 * (r + x + y) for r, x, y in moved], a)

        rows(1, ROWS - 1, third)
        rows(2, ROWS - 2, second)
        rows(3, ROWS - 3, finish)

        for copy in back:
            copy.wait_recv()

        def edge_adjoint(a):
            m = get(m01, a)
            for comp, rd in ((0, rdu), (1, rdv)):
                p = [r * x for r, x in zip(get(rd, a), get(l4, a, comp))]
                put(p4, p, a, comp)
                put(q4, [x * y for x, y in zip(m, p)], a, comp)

        rows(-3, 0, edge_adjoint)
        rows(ROWS, ROWS + 3, edge_adjoint)
        for a in (0, HELD - 1):
            for comp in (0, 1):
                put(q4, [x * y for x, y in zip(get(m01, a), get(p4, a, comp))], a, comp)
        rows(-3, 1, third)
        rows(ROWS - 1, ROWS + 3, third)
        rows(-2, 2, second)
        rows(ROWS - 2, ROWS + 2, second)
        rows(-1, 3, finish)
        rows(ROWS - 3, ROWS + 1, finish)
        for k in every:
            at = (OFF - 1, slice(None), lanes(k))
            faces[at] = faces[at] + has_up * g4in[0, :, lanes(k)]
            at = (OFF + ROWS, slice(None), lanes(k))
            facen[at] = facen[at] + has_down * g4in[1, :, lanes(k)]

        def gradients(a):
            i = a - OFF
            for k in every:
                at = (slice(None), lanes(k))
                grad[(i, *at)] = -fric[(a, *at)] * accu[(a, *at)]
                both = own[(a, *at)] + 0.5 * (faces[(a - 1, *at)] + facen[(a + 1, *at)])
                grad[(i + ROWS, *at)] = stiff[(a, *at)] * both

        rows(0, ROWS, gradients)

        order = list(reversed(range(len(peers))))
        scatter = [
            send(grad.at[peers[k]], rsbuf.at[k], rsend.at[k], rrecv.at[k], {"epoch": peers[k]})
            for k in order
        ]
        mine = get(grad, ep)
        for copy, k in zip(scatter, order):
            copy.wait_recv()
            mine = [x + y for x, y in zip(mine, get(rsbuf, k))]
        put(total, mine, ep)
        put(summed, mine)
        sq = mine[0] * mine[0]
        for k in range(1, pieces):
            sq = sq + mine[k] * mine[k]
        sq = jnp.sum(sq, axis=0, keepdims=True)
        sqout[...] = sq
        sqin[ep] = sq

        squares = [
            send(sqout, sqin.at[ep], ssend.at[k], srecv.at[k], {"epoch": peers[k]}) for k in order
        ]
        gather = [
            send(summed, total.at[ep], gsend.at[k], grecv.at[k], {"epoch": peers[k]}) for k in order
        ]
        for copy in squares:
            copy.wait_recv()
        tot_q, tot_r = sqin[0], sqin[n_epoch // 2]
        for k in range(1, n_epoch // 2):
            tot_q = tot_q + sqin[k]
            tot_r = tot_r + sqin[n_epoch // 2 + k]
        rowout[0] = tot_q
        rowout[1] = tot_r
        across = [
            send(rowout, rowin.at[k - 1], tsend.at[k - 1], trecv.at[k - 1], {"row": lax.rem(me + k, n_row)})
            for k in range(1, n_row)
        ]
        for k, copy in enumerate(across):
            copy.wait_recv()
            tot_q = tot_q + rowin[k, 0]
            tot_r = tot_r + rowin[k, 1]
        factors = []
        for tot in (tot_q, tot_r):
            mean = jnp.sum(tot, axis=1, keepdims=True) / cells
            factor = step_size / jnp.sqrt(mean + 1e-6)
            factors.append(jnp.broadcast_to(factor, (SUB, LANE)))
        for copy in gather:
            copy.wait_recv()

        def update(a):
            i = a - OFF
            for ref, old, shift, factor in (
                (outq, lfraw, 0, factors[0]), (outr, lrraw, ROWS, factors[1])
            ):
                g = get(total, i + shift)
                for k in every:
                    at = (pl.ds(k * SUB + i, SUB, stride=span), slice(None))
                    ref[at] = old[at] - factor * g[k]

        rows(0, ROWS, update)

        for copy in halo + back + scatter + squares + gather + across:
            copy.wait_send()

    return kernel


def tiles(x):
    lead = x.shape[:-2]
    x = x.reshape(*lead, ROWS, x.shape[-1] // LANE, LANE)
    return jnp.swapaxes(x, -2, -3).reshape(-1, LANE)


def solution(mesh):
    n_epoch, n_row = mesh.shape["epoch"], mesh.shape["row"]

    def on_device(forcing, observed, log_friction, log_rheology, grounded):
        cols = forcing.shape[-1]
        width = cols // SUB
        raw_rows = ROWS * cols // LANE
        row = pltpu.VMEM((HELD, SUB, width), jnp.float32)
        pair = pltpu.VMEM((HELD, 2, SUB, width), jnp.float32)
        plain = lambda *lead: pltpu.VMEM((*lead, SUB, width), jnp.float32)
        dma = lambda n: pltpu.SemaphoreType.DMA((n,))
        scratch = [
            pltpu.VMEM((2 * raw_rows, LANE), jnp.float32),
            pltpu.VMEM((2 * raw_rows, LANE), jnp.float32),
            pltpu.VMEM((raw_rows, LANE), jnp.float32),
            pltpu.VMEM((raw_rows, LANE), jnp.float32),
            pltpu.VMEM((raw_rows, LANE), jnp.int32),
            row, row, pair, row, row, row, row, row, row, row,
            pair, pair, pair, pair,
            *([pair] * 9),
            *([row] * 7),
            row, row, row, plain(n_epoch), plain(2), plain(2),
            plain(n_epoch - 1), plain(), plain(n_epoch),
            pltpu.VMEM((1, LANE), jnp.float32),
            pltpu.VMEM((n_epoch, 1, LANE), jnp.float32),
            pltpu.VMEM((2, 1, LANE), jnp.float32),
            pltpu.VMEM((n_row - 1, 2, 1, LANE), jnp.float32),
            dma(5), dma(6), dma(6), dma(6), dma(6),
            *([dma(n_epoch - 1)] * 6),
            *([dma(n_row - 1)] * 2),
        ]
        shape = jax.ShapeDtypeStruct((raw_rows, LANE), jnp.float32)
        outs = pl.pallas_call(
            make_kernel(n_epoch, n_row, cols),
            out_shape=(shape, shape),
            in_specs=[pl.BlockSpec(memory_space=pl.ANY)] * 5,
            out_specs=(pl.BlockSpec(memory_space=pltpu.VMEM),) * 2,
            scratch_shapes=scratch,
            compiler_params=pltpu.CompilerParams(
                collective_id=0, has_side_effects=True, vmem_limit_bytes=60 * 2**20
            ),
            name="inversion_step",
        )(*(tiles(x) for x in (forcing, observed, log_friction, log_rheology, grounded)))

        def whole(x):
            return jnp.swapaxes(x.reshape(cols // LANE, ROWS, LANE), 0, 1).reshape(ROWS, cols)

        return whole(outs[0]), whole(outs[1])

    in_specs = (
        P("epoch", None, "row", None),
        P("epoch", None, "row", None),
        P("row", None),
        P("row", None),
        P("row", None),
    )
    out_specs = (P("row", None), P("row", None))
    return jax.shard_map(
        on_device, mesh=mesh, in_specs=in_specs, out_specs=out_specs, check_vma=False
    )
```

```python
import math

import jax
import jax.numpy as jnp
from jax import lax
from jax.experimental import pallas as pl
from jax.experimental.pallas import tpu as pltpu
from jax.sharding import PartitionSpec as P

relax = 0.9
coupling = 0.1
step_size = 0.5
keep = 1.0 - relax

MESH = pl.DeviceIdType.MESH
ROWS = 8
OFF = 4
HELD = ROWS + 2 * OFF
SUB, LANE = 8, 128


def make_kernel(n_epoch, n_row, cols):
    pieces = cols // (SUB * LANE)
    span = pieces * SUB
    side = math.isqrt(n_epoch)
    cells = n_row * ROWS * cols

    def kernel(
        f_in, o_in, lf_in, lr_in, gr_in, outq, outr,
        fraw, oraw, lfraw, lrraw, grraw,
        stiff, fric, force, fe, fw, fn, fs, m01, rdu, rdv,
        v1, v2, v3, v4,
        l4, p4, q4, l3, p3, q3, l2, p2, q2,
        accn, accs, acce, accw, accc, accu, accv,
        facen, faces, own, grad, g4out, g4in,
        rsbuf, summed, total, sqout, sqin, rowout, rowin,
        load_sem, hsend, hrecv, asend, arecv, rsend, rrecv, gsend, grecv, ssend, srecv, tsend, trecv,
    ):
        me = lax.axis_index("row")
        ep = lax.axis_index("epoch")
        up = lax.rem(me + n_row - 1, n_row)
        down = lax.rem(me + 1, n_row)
        has_up = (me > 0).astype(jnp.float32)
        has_down = (me < n_row - 1).astype(jnp.float32)

        loads = [
            pltpu.make_async_copy(src, dst, load_sem.at[k])
            for k, (src, dst) in enumerate(
                ((lr_in, lrraw), (lf_in, lfraw), (gr_in, grraw), (f_in, fraw), (o_in, oraw))
            )
        ]
        for load in loads:
            load.start()

        ex, ey = ep // side, lax.rem(ep, side)
        peers = []
        for dx in range(side):
            for dy in range(side):
                if dx or dy:
                    peers.append(lax.rem(ex + dx, side) * side + lax.rem(ey + dy, side))

        barrier = pltpu.get_barrier_semaphore()
        for k in range(1, n_row):
            pl.semaphore_signal(
                barrier, inc=1, device_id={"row": lax.rem(me + k, n_row)}, device_id_type=MESH
            )
        for peer in peers:
            pl.semaphore_signal(barrier, inc=1, device_id={"epoch": peer}, device_id_type=MESH)

        lane = lax.broadcasted_iota(jnp.int32, (SUB, LANE), 1)
        sub = lax.broadcasted_iota(jnp.int32, (SUB, LANE), 0)
        last_lane, first_lane = lane == LANE - 1, lane == 0
        last_sub, first_sub = sub == SUB - 1, sub == 0
        zero = jnp.zeros((SUB, LANE), jnp.float32)
        every = range(pieces)

        def east(x):
            r = [pltpu.roll(p, LANE - 1, 1) for p in x]
            end = jnp.where(last_sub, zero, pltpu.roll(r[0], SUB - 1, 0))
            return [jnp.where(last_lane, r[k + 1] if k + 1 < pieces else end, r[k]) for k in every]

        def west(x):
            r = [pltpu.roll(p, 1, 1) for p in x]
            end = jnp.where(first_sub, zero, pltpu.roll(r[-1], 1, 0))
            return [jnp.where(first_lane, r[k - 1] if k else end, r[k]) for k in every]

        def lanes(k):
            return slice(k * LANE, (k + 1) * LANE)

        def get(ref, *at):
            return [ref[(*at, slice(None), lanes(k))] for k in every]

        def put(ref, x, *at):
            for k in every:
                ref[(*at, slice(None), lanes(k))] = x[k]

        def raw(ref, i, part=0):
            return [ref[pl.ds(part * span * SUB + k * SUB + i, SUB, stride=span), :] for k in every]

        def cross(north, south):
            d = [s - n for s, n in zip(south, north)]
            return [a - b for a, b in zip(east(d), west(d))]

        def rows(lo, hi, body, by=2):
            by = by if (hi - lo) % by == 0 else 1

            def step(n, carry):
                for m in range(by):
                    body(lo + OFF + n * by + m)
                return carry

            lax.fori_loop(0, (hi - lo) // by, step, 0)

        loads[0].wait()

        def own_stiff(a):
            put(stiff, [jnp.exp(x) for x in raw(lrraw, a - OFF)], a)

        rows(0, ROWS, own_stiff, 4)
        loads[1].wait()
        loads[2].wait()

        def own_fric(a):
            held_up = zip(raw(grraw, a - OFF), raw(lfraw, a - OFF))
            put(fric, [g.astype(jnp.float32) * jnp.exp(x) for g, x in held_up], a)

        rows(0, ROWS, own_fric, 4)
        loads[3].wait()

        def own_force(a):
            put(force, raw(fraw, a - OFF, 0), a, 0)
            put(force, raw(fraw, a - OFF, 1), a, 1)

        rows(0, ROWS, own_force, 4)

        pl.semaphore_wait(barrier, n_row - 1 + len(peers))

        def send(src, dst, ssem, rsem, where):
            copy = pltpu.make_async_remote_copy(
                src_ref=src, dst_ref=dst, send_sem=ssem, recv_sem=rsem,
                device_id=where, device_id_type=MESH,
            )
            copy.start()
            return copy

        halo = []
        for k, (ref, depth) in enumerate(((stiff, 4), (fric, 3), (force, 3))):
            halo.append(send(
                ref.at[pl.ds(OFF, depth)], ref.at[pl.ds(OFF + ROWS, depth)],
                hsend.at[2 * k], hrecv.at[2 * k], {"row": up},
            ))
            halo.append(send(
                ref.at[pl.ds(OFF + ROWS - depth, depth)], ref.at[pl.ds(OFF - depth, depth)],
                hsend.at[2 * k + 1], hrecv.at[2 * k + 1], {"row": down},
            ))

        def coefficients(a):
            c, n, s = get(stiff, a), get(stiff, a - 1), get(stiff, a + 1)
            he = [0.5 * (x + y) for x, y in zip(c, east(c))]
            hw = [0.5 * (x + y) for x, y in zip(c, west(c))]
            hn = [0.5 * (x + y) for x, y in zip(c, n)]
            hs = [0.5 * (x + y) for x, y in zip(c, s)]
            fr = get(fric, a)
            inside = relax * jnp.where(a < OFF, has_up, jnp.where(a >= OFF + ROWS, has_down, 1.0))
            put(fe, he, a)
            put(fw, hw, a)
            put(fn, hn, a)
            put(fs, hs, a)
            put(m01, [coupling * x for x in c], a)
            fu, fv = get(force, a, 0), get(force, a, 1)
            for k in every:
                along, across = he[k] + hw[k], hn[k] + hs[k]
                base = fr[k] + 0.5
                ru = inside / (4.0 * along + across + base)
                rv = inside / (along + 4.0 * across + base)
                rdu[a, :, lanes(k)] = ru
                rdv[a, :, lanes(k)] = rv
                v1[a, 0, :, lanes(k)] = ru * fu[k]
                v1[a, 1, :, lanes(k)] = rv * fv[k]

        def sweep(src, dst):
            def body(a):
                he, hw, hn, hs, m = get(fe, a), get(fw, a), get(fn, a), get(fs, a), get(m01, a)
                un, uc, us = get(src, a - 1, 0), get(src, a, 0), get(src, a + 1, 0)
                vn, vc, vs = get(src, a - 1, 1), get(src, a, 1), get(src, a + 1, 1)
                ue, uw, ve, vw = east(uc), west(uc), east(vc), west(vc)
                xu, xv = cross(un, us), cross(vn, vs)
                for k in every:
                    lat_u = he[k] * ue[k] + hw[k] * uw[k]
                    ver_u = hn[k] * un[k] + hs[k] * us[k]
                    lat_v = he[k] * ve[k] + hw[k] * vw[k]
                    ver_v = hn[k] * vn[k] + hs[k] * vs[k]
                    off_u = 4.0 * lat_u + ver_u + m[k] * xv[k]
                    off_v = lat_v + 4.0 * ver_v + m[k] * xu[k]
                    at = (slice(None), lanes(k))
                    dst[(a, 0, *at)] = keep * uc[k] + v1[(a, 0, *at)] + rdu[(a, *at)] * off_u
                    dst[(a, 1, *at)] = keep * vc[k] + v1[(a, 1, *at)] + rdv[(a, *at)] * off_v

            return body

        rows(1, ROWS - 1, coefficients)
        rows(2, ROWS - 2, sweep(v1, v2))
        rows(3, ROWS - 3, sweep(v2, v3))

        for copy in halo:
            copy.wait_recv()
        for k in every:
            stiff[OFF - 1, :, lanes(k)] = stiff[OFF - 1, :, lanes(k)] * has_up
            stiff[OFF + ROWS, :, lanes(k)] = stiff[OFF + ROWS, :, lanes(k)] * has_down
        rows(-3, 1, coefficients)
        rows(ROWS - 1, ROWS + 3, coefficients)
        for a in (0, HELD - 1):
            put(m01, [coupling * x for x in get(stiff, a)], a)
        rows(-2, 2, sweep(v1, v2))
        rows(ROWS - 2, ROWS + 2, sweep(v1, v2))
        rows(-1, 3, sweep(v2, v3))
        rows(ROWS - 3, ROWS + 1, sweep(v2, v3))
        rows(0, ROWS, sweep(v3, v4))

        loads[4].wait()

        def last_adjoint(a):
            m = get(m01, a)
            for comp, rd in ((0, rdu), (1, rdv)):
                lam = [x - y for x, y in zip(get(v4, a, comp), raw(oraw, a - OFF, comp))]
                p = [r * x for r, x in zip(get(rd, a), lam)]
                put(l4, lam, a, comp)
                put(p4, p, a, comp)
                put(q4, [x * y for x, y in zip(m, p)], a, comp)

        rows(0, ROWS, last_adjoint, 4)
        back = [
            send(l4.at[pl.ds(OFF, 3)], l4.at[pl.ds(OFF + ROWS, 3)], asend.at[0], arecv.at[0], {"row": up}),
            send(l4.at[pl.ds(OFF + ROWS - 3, 3)], l4.at[pl.ds(OFF - 3, 3)], asend.at[1], arecv.at[1], {"row": down}),
            send(p4.at[pl.ds(OFF + 3, 1)], p4.at[pl.ds(OFF + ROWS + 3, 1)], asend.at[2], arecv.at[2], {"row": up}),
            send(p4.at[pl.ds(OFF + ROWS - 4, 1)], p4.at[pl.ds(0, 1)], asend.at[3], arecv.at[3], {"row": down}),
        ]

        def terms(a, p, before, after):
            pu, pv = get(p, a, 0), get(p, a, 1)
            un, uc, us = get(before, a - 1, 0), get(before, a, 0), get(before, a + 1, 0)
            vn, vc, vs = get(before, a - 1, 1), get(before, a, 1), get(before, a + 1, 1)
            ue, uw, ve, vw = east(uc), west(uc), east(vc), west(vc)
            xu, xv = cross(un, us), cross(vn, vs)
            au, av = get(after, a, 0), get(after, a, 1)
            out = []
            for k in every:
                pu4, pv4 = 4.0 * pu[k], 4.0 * pv[k]
                out.append((
                    pu[k] * un[k] + pv4 * vn[k],
                    pu[k] * us[k] + pv4 * vs[k],
                    pu4 * ue[k] + pv[k] * ve[k],
                    pu4 * uw[k] + pv[k] * vw[k],
                    pu[k] * xv[k] + pv[k] * xu[k],
                    pu[k] * (au[k] - keep * uc[k]),
                    pv[k] * (av[k] - keep * vc[k]),
                ))
            return out

        held = (accn, accs, acce, accw, accc, accu, accv)

        def last_terms(a):
            for k, values in enumerate(terms(a, p4, v3, v4)):
                for ref, value in zip(held, values):
                    ref[a, :, lanes(k)] = value

        rows(0, ROWS, last_terms)
        inv = 1.0 / relax
        for k in every:
            for slot, (a, ref) in enumerate(((OFF, accn), (OFF + ROWS - 1, accs))):
                at = (a, slice(None), lanes(k))
                g4out[slot, :, lanes(k)] = ref[at] - inv * (accu[at] + 4.0 * accv[at])
            for a in (OFF - 1, OFF + ROWS):
                for ref in held:
                    ref[a, :, lanes(k)] = zero
        back.append(send(g4out.at[0], g4in.at[1], asend.at[4], arecv.at[4], {"row": up}))
        back.append(send(g4out.at[1], g4in.at[0], asend.at[5], arecv.at[5], {"row": down}))

        def adjoint_row(a, lam, p, q):
            he, hw, hn, hs = get(fe, a), get(fw, a), get(fn, a), get(fs, a)
            result = []
            for comp, (along, across) in enumerate(((4.0, 1.0), (1.0, 4.0))):
                pn, pc, ps = get(p, a - 1, comp), get(p, a, comp), get(p, a + 1, comp)
                pe, pw = east(pc), west(pc)
                x = cross(get(q, a - 1, 1 - comp), get(q, a + 1, 1 - comp))
                la = get(lam, a, comp)
                new = []
                for k in every:
                    lat = he[k] * pe[k] + hw[k] * pw[k]
                    ver = hn[k] * pn[k] + hs[k] * ps[k]
                    lat = 4.0 * lat if comp == 0 else lat
                    ver = 4.0 * ver if comp == 1 else ver
                    new.append(keep * la[k] + lat + ver + x[k])
                result.append(new)
            return result

        def adjoint(lam, p, q, lam_to, p_to, q_to):
            def body(a):
                m = get(m01, a)
                for comp, (new, rd) in enumerate(zip(adjoint_row(a, lam, p, q), (rdu, rdv))):
                    pp = [r * x for r, x in zip(get(rd, a), new)]
                    put(lam_to, new, a, comp)
                    put(p_to, pp, a, comp)
                    put(q_to, [x * y for x, y in zip(m, pp)], a, comp)

            return body

        third = adjoint(l4, p4, q4, l3, p3, q3)
        second = adjoint(l3, p3, q3, l2, p2, q2)

        def finish(a):
            t3, t2 = terms(a, p3, v2, v3), terms(a, p2, v1, v2)
            l1 = adjoint_row(a, l2, p2, q2)
            east_part, west_part, rest = [], [], []
            for k in every:
                at = (a, slice(None), lanes(k))
                tn, ts, te, tw, tc, tu, tv = (
                    ref[at] + x + y for ref, x, y in zip(held, t3[k], t2[k])
                )
                tu = inv * (tu + rdu[at] * l1[0][k] * v1[(a, 0, *at[1:])])
                tv = inv * (tv + rdv[at] * l1[1][k] * v1[(a, 1, *at[1:])])
                wide, tall = 4.0 * tu + tv, tu + 4.0 * tv
                tn, ts, te, tw = tn - tall, ts - tall, te - wide, tw - wide
                facen[at] = tn
                faces[at] = ts
                accu[at] = tu + tv
                east_part.append(te)
                west_part.append(tw)
                rest.append(tn + ts + te + tw + (2.0 * coupling) * tc)
            moved = zip(rest, east(west_part), west(east_part))
            put(own, [0.5 * (r + x + y) for r, x, y in moved], a)

        rows(1, ROWS - 1, third)
        rows(2, ROWS - 2, second)
        rows(3, ROWS - 3, finish)

        for copy in back:
            copy.wait_recv()

        def edge_adjoint(a):
            m = get(m01, a)
            for comp, rd in ((0, rdu), (1, rdv)):
                p = [r * x for r, x in zip(get(rd, a), get(l4, a, comp))]
                put(p4, p, a, comp)
                put(q4, [x * y for x, y in zip(m, p)], a, comp)

        rows(-3, 0, edge_adjoint)
        rows(ROWS, ROWS + 3, edge_adjoint)
        for a in (0, HELD - 1):
            for comp in (0, 1):
                put(q4, [x * y for x, y in zip(get(m01, a), get(p4, a, comp))], a, comp)
        rows(-3, 1, third)
        rows(ROWS - 1, ROWS + 3, third)
        rows(-2, 2, second)
        rows(ROWS - 2, ROWS + 2, second)
        rows(-1, 3, finish)
        rows(ROWS - 3, ROWS + 1, finish)
        for k in every:
            at = (OFF - 1, slice(None), lanes(k))
            faces[at] = faces[at] + has_up * g4in[0, :, lanes(k)]
            at = (OFF + ROWS, slice(None), lanes(k))
            facen[at] = facen[at] + has_down * g4in[1, :, lanes(k)]

        def gradients(a):
            i = a - OFF
            for k in every:
                at = (slice(None), lanes(k))
                grad[(i, *at)] = -fric[(a, *at)] * accu[(a, *at)]
                both = own[(a, *at)] + 0.5 * (faces[(a - 1, *at)] + facen[(a + 1, *at)])
                grad[(i + ROWS, *at)] = stiff[(a, *at)] * both

        rows(0, ROWS, gradients, 4)

        order = list(reversed(range(len(peers))))
        scatter = [
            send(grad.at[peers[k]], rsbuf.at[k], rsend.at[k], rrecv.at[k], {"epoch": peers[k]})
            for k in order
        ]
        mine = get(grad, ep)
        for copy, k in zip(scatter, order):
            copy.wait_recv()
            mine = [x + y for x, y in zip(mine, get(rsbuf, k))]
        put(total, mine, ep)
        put(summed, mine)
        sq = mine[0] * mine[0]
        for k in range(1, pieces):
            sq = sq + mine[k] * mine[k]
        sq = jnp.sum(sq, axis=0, keepdims=True)
        sqout[...] = sq
        sqin[ep] = sq

        squares = [
            send(sqout, sqin.at[ep], ssend.at[k], srecv.at[k], {"epoch": peers[k]}) for k in order
        ]
        gather = [
            send(summed, total.at[ep], gsend.at[k], grecv.at[k], {"epoch": peers[k]}) for k in order
        ]
        for copy in squares:
            copy.wait_recv()
        tot_q, tot_r = sqin[0], sqin[n_epoch // 2]
        for k in range(1, n_epoch // 2):
            tot_q = tot_q + sqin[k]
            tot_r = tot_r + sqin[n_epoch // 2 + k]
        rowout[0] = tot_q
        rowout[1] = tot_r
        across = [
            send(rowout, rowin.at[k - 1], tsend.at[k - 1], trecv.at[k - 1], {"row": lax.rem(me + k, n_row)})
            for k in range(1, n_row)
        ]
        for k, copy in enumerate(across):
            copy.wait_recv()
            tot_q = tot_q + rowin[k, 0]
            tot_r = tot_r + rowin[k, 1]
        factors = []
        for tot in (tot_q, tot_r):
            mean = jnp.sum(tot, axis=1, keepdims=True) / cells
            factor = step_size / jnp.sqrt(mean + 1e-6)
            factors.append(jnp.broadcast_to(factor, (SUB, LANE)))
        for copy in gather:
            copy.wait_recv()

        def update(a):
            i = a - OFF
            for ref, old, shift, factor in (
                (outq, lfraw, 0, factors[0]), (outr, lrraw, ROWS, factors[1])
            ):
                g = get(total, i + shift)
                for k in every:
                    at = (pl.ds(k * SUB + i, SUB, stride=span), slice(None))
                    ref[at] = old[at] - factor * g[k]

        rows(0, ROWS, update, 4)

        for copy in halo + back + scatter + squares + gather + across:
            copy.wait_send()

    return kernel


def tiles(x):
    lead = x.shape[:-2]
    x = x.reshape(*lead, ROWS, x.shape[-1] // LANE, LANE)
    return jnp.swapaxes(x, -2, -3).reshape(-1, LANE)


def solution(mesh):
    n_epoch, n_row = mesh.shape["epoch"], mesh.shape["row"]

    def on_device(forcing, observed, log_friction, log_rheology, grounded):
        cols = forcing.shape[-1]
        width = cols // SUB
        raw_rows = ROWS * cols // LANE
        row = pltpu.VMEM((HELD, SUB, width), jnp.float32)
        pair = pltpu.VMEM((HELD, 2, SUB, width), jnp.float32)
        plain = lambda *lead: pltpu.VMEM((*lead, SUB, width), jnp.float32)
        dma = lambda n: pltpu.SemaphoreType.DMA((n,))
        scratch = [
            pltpu.VMEM((2 * raw_rows, LANE), jnp.float32),
            pltpu.VMEM((2 * raw_rows, LANE), jnp.float32),
            pltpu.VMEM((raw_rows, LANE), jnp.float32),
            pltpu.VMEM((raw_rows, LANE), jnp.float32),
            pltpu.VMEM((raw_rows, LANE), jnp.int32),
            row, row, pair, row, row, row, row, row, row, row,
            pair, pair, pair, pair,
            *([pair] * 9),
            *([row] * 7),
            row, row, row, plain(n_epoch), plain(2), plain(2),
            plain(n_epoch - 1), plain(), plain(n_epoch),
            pltpu.VMEM((1, LANE), jnp.float32),
            pltpu.VMEM((n_epoch, 1, LANE), jnp.float32),
            pltpu.VMEM((2, 1, LANE), jnp.float32),
            pltpu.VMEM((n_row - 1, 2, 1, LANE), jnp.float32),
            dma(5), dma(6), dma(6), dma(6), dma(6),
            *([dma(n_epoch - 1)] * 6),
            *([dma(n_row - 1)] * 2),
        ]
        shape = jax.ShapeDtypeStruct((raw_rows, LANE), jnp.float32)
        outs = pl.pallas_call(
            make_kernel(n_epoch, n_row, cols),
            out_shape=(shape, shape),
            in_specs=[pl.BlockSpec(memory_space=pl.ANY)] * 5,
            out_specs=(pl.BlockSpec(memory_space=pltpu.VMEM),) * 2,
            scratch_shapes=scratch,
            compiler_params=pltpu.CompilerParams(
                collective_id=0, has_side_effects=True, vmem_limit_bytes=60 * 2**20
            ),
            name="inversion_step",
        )(*(tiles(x) for x in (forcing, observed, log_friction, log_rheology, grounded)))

        def whole(x):
            return jnp.swapaxes(x.reshape(cols // LANE, ROWS, LANE), 0, 1).reshape(ROWS, cols)

        return whole(outs[0]), whole(outs[1])

    in_specs = (
        P("epoch", None, "row", None),
        P("epoch", None, "row", None),
        P("row", None),
        P("row", None),
        P("row", None),
    )
    out_specs = (P("row", None), P("row", None))
    return jax.shard_map(
        on_device, mesh=mesh, in_specs=in_specs, out_specs=out_specs, check_vma=False
    )
```
